512 devices in a mesh: frames: 64 (over y, x, core), coils: 8 (over z).
Axes of the slice: x: 4, y: 8, z: 8, core: 2. Of those that a mesh axis runs over, the one named last changes fastest.
Arguments:
- kspace: bfloat16 [64, 32, 2, 32, 256], P('frames', 'coils'), may hold values from -6 to 6
- sensitivity: bfloat16 [32, 2, 256, 256], P('coils'), may hold values from -3 to 3
- spoke_count: int32 [64], P('frames'), may hold values from 1 to 32, 1536 in all
- spoke_index: int32 [64, 32], P('frames'), may hold values from 0 to 32767
- band_offset: int32 [64, 32], P('frames'), may hold values from 0 to 252
- owner_map: int32 [8, 8192], replicated, may hold values from 0 to 8191, each once within a row
- aif: float32 [64], replicated, may hold values from 0.2 to 5
- ktrans: float32 [8, 8192], P('coils', 'frames'), may hold values from 0.02 to 0.4
- kep: float32 [8, 8192], P('coils', 'frames'), may hold values from 0.1 to 2
- baseline: float32 [2, 8, 8192], P(None, 'coils', 'frames'), may hold values from 0.5 to 2
Outputs:
- ktrans_new: float32 [8, 8192], P('coils', 'frames')
- kep_new: float32 [8, 8192], P('coils', 'frames')
- residual_images: bfloat16 [64, 2, 256, 256], P('frames', None, 'coils')
The draws below stay inside these ranges and needn't reach their ends.
Inputs may be any that keep to these rules, and one draw needn't show every extreme that they name: `spoke_count`: spoke counts of all frames sum to 1536; some frame uses all 32 slots. `owner_map`: each row is a permutation of 0 to 8191.
All inputs are finite; a program needn't handle non-finite values. No bound on the sum of `spoke_count` on one device may be relied on, other than what follows from the above.
Results may differ from the reference program's by a relative error of at most 0.0074.
Values may be sent and summed in bfloat16 or wider, within the bound.
No kernel may reach another device: no remote copies, remote signals or barrier semaphores. Data moves between devices by JAX's collectives and lax.ppermute only.
A program may use at most 64 MiB of HBM per device.

```python
import math
import jax
import jax.numpy as jnp
import numpy as np
from jax import lax

NX = 256
SPK = 32
BAND = 4
FRAMES = 64
COILS = 32
SLAB_VOX = 8192
SPOKE_TOTAL = 1536
N_COILS = 8


def place_ends(values, rng, least, high):
    spot = [jax.random.randint(jax.random.fold_in(rng, axis), (), 0, length) for axis, length in enumerate(values.shape)]
    longest = values.shape.index(max(values.shape))
    neighbour = spot[:longest] + [(spot[longest] + 1) % values.shape[longest]] + spot[longest + 1:]
    return values.at[tuple(spot)].set(least).at[tuple(neighbour)].set(high)


def levels(rng, dims, shards, least, largest):
    loudness = 1.0
    for axis_at, parts in shards:
        steps = jax.random.uniform(jax.random.fold_in(jax.random.fold_in(rng, 6), axis_at), (parts,), jnp.float32, least / len(shards), largest / len(shards))
        loudness = loudness * jnp.repeat(jnp.exp(steps), dims[axis_at] // parts).reshape((-1,) + (1,) * (len(dims) - 1 - axis_at))
    return loudness


def length_profile(number_of, total, most, skew):
    loads = [(1 << 20) // math.isqrt(grade ** skew) + 1 for grade in range(2, number_of + 1)]
    surplus, counts = total - most - (number_of - 1), [1] * (number_of - 1)
    while surplus > 0:
        movable = [i for i in range(number_of - 1) if counts[i] < most]
        mass, budget = sum([loads[i] for i in movable]), surplus
        for i in movable:
            more = min(most - counts[i], max(1, budget * loads[i] // mass), surplus)
            counts[i] = counts[i] + more
            surplus = surplus - more
    return np.array([most] + counts)


def uneven(key, number_of, total, limit, lean):
    if number_of == 2:
        one = jax.random.randint(key, (), max(1, total - limit), min(limit, total - 1) + 1)
        return jnp.stack([one, total - one])
    tallies = jnp.asarray(length_profile(number_of, total, limit, lean), jnp.int32)
    twos = (number_of - 1) // 2
    donor, sink = tallies[1:1 + 2 * twos:2], tallies[2:2 + 2 * twos:2]
    margin = jnp.minimum(donor - 1, limit - sink)
    moved = jax.random.randint(jax.random.fold_in(key, 1), (twos,), 0, 1 << 20) % (margin + 1)
    tallies = tallies.at[1:1 + 2 * twos:2].set(donor - moved).at[2:2 + 2 * twos:2].set(sink + moved)
    return tallies[jax.random.permutation(jax.random.fold_in(key, 2), number_of)]


def scatter_about(key, extent, width, limit, cuts=(), kind=jnp.bfloat16):
    factor_of = levels(key, extent, cuts, -0.22, 0.18) if cuts else 1.0
    result = jax.random.normal(key, extent, jnp.float32) * width * factor_of
    return jnp.minimum(jnp.maximum(result, -limit), limit).astype(kind)


def setup_inputs(seed: int = 0) -> dict:
    arg_keys = jax.random.split(jax.random.key(seed), 11)
    kspace = scatter_about(arg_keys[0], (FRAMES, COILS, 2, SPK, NX), 1.0, 6.0, ((0, 64), (1, 8)))
    sensitivity = scatter_about(arg_keys[1], (COILS, 2, NX, NX), 0.5, 3.0, ((0, 8),))
    spoke_count = uneven(arg_keys[2], FRAMES, SPOKE_TOTAL, SPK, 2).astype(jnp.int32)
    spoke_index = place_ends(jax.random.randint(arg_keys[3], (FRAMES, SPK), 0, 32768), jax.random.fold_in(arg_keys[3], 1), 0, 32767).astype(jnp.int32)
    band_offset = place_ends(jax.random.randint(arg_keys[4], (FRAMES, SPK), 0, NX - BAND + 1), jax.random.fold_in(arg_keys[4], 1), 0, NX - BAND).astype(jnp.int32)
    owner_map = jax.vmap(lambda own: jax.random.permutation(own, SLAB_VOX))(jax.random.split(arg_keys[5], N_COILS)).reshape((N_COILS, SLAB_VOX)).astype(jnp.int32)
    aif = jnp.clip(jnp.exp(jax.random.uniform(arg_keys[6], (FRAMES,), jnp.float32, math.log(0.2), math.log(5.0))), 0.2, 5.0)
    ktrans = jnp.clip(jnp.exp(math.log(0.4) - 2.9957323 * jax.random.uniform(arg_keys[7], (N_COILS, SLAB_VOX), jnp.float32) ** levels(arg_keys[7], (N_COILS, SLAB_VOX), ((0, 8), (1, 64)), -0.2, 0.2)), 0.02, 0.4)
    kep = jnp.clip(jnp.exp(math.log(2.0) - 2.9957323 * jax.random.uniform(arg_keys[8], (N_COILS, SLAB_VOX), jnp.float32) ** levels(arg_keys[8], (N_COILS, SLAB_VOX), ((0, 8), (1, 64)), -0.2, 0.2)), 0.1, 2.0)
    baseline = jnp.clip(0.5 + 1.5 * jax.random.uniform(arg_keys[9], (2, N_COILS, SLAB_VOX), jnp.float32) ** levels(arg_keys[9], (2, N_COILS, SLAB_VOX), ((1, 8), (2, 64)), -0.2, 0.2), 0.5, 2.0)
    return dict(kspace=kspace, sensitivity=sensitivity, spoke_count=spoke_count, spoke_index=spoke_index, band_offset=band_offset, owner_map=owner_map, aif=aif, ktrans=ktrans, kep=kep, baseline=baseline)


KERNEL = (0.25, 0.75, 0.75, 0.25)
STEP_MINUTES = 0.05
DAMPING = 0.1

def dft_tables(length):
    index = jnp.arange(length, dtype=jnp.int32)
    phase = (index[:, None] * index[None, :] % length).astype(jnp.float32) * (2.0 * math.pi / length)
    norm = 1.0 / math.sqrt(length)
    cosine = (jnp.cos(phase) * norm).astype(jnp.bfloat16)
    sine = (jnp.sin(phase) * norm).astype(jnp.bfloat16)
    column_table = jnp.stack([jnp.stack([cosine, sine], 1), jnp.stack([-sine, cosine], 1)], 0)
    row_table = jnp.stack([jnp.stack([cosine, -sine], 1), jnp.stack([sine, cosine], 1)], 0)
    return (column_table, row_table)

def spoke_weights(count, offset, spoke_number, rows):
    spokes = offset.shape[0]
    row_ids = jnp.arange(rows, dtype=jnp.int32)
    band = jnp.zeros((rows, spokes), jnp.float32)
    for shift_b in range(len(KERNEL)):
        band = band + KERNEL[shift_b] * (row_ids[:, None] == offset[None, :] + shift_b).astype(jnp.float32)
    live = (jnp.arange(spokes, dtype=jnp.int32) < count).astype(jnp.float32)
    turn = (spoke_number * 40503 % 65536).astype(jnp.float32) * (2.0 * math.pi / 65536.0)
    w_cos = band * (live * jnp.cos(turn))[None, :]
    w_sin = band * (live * jnp.sin(turn))[None, :]
    return jnp.stack([jnp.stack([w_cos, -w_sin], 1), jnp.stack([w_sin, w_cos], 1)], 0).astype(jnp.bfloat16)

def aif_matrix(aif):
    length = aif.shape[0]
    index = jnp.arange(length, dtype=jnp.int32)
    lag = index[:, None] - index[None, :]
    table = jnp.take(aif, jnp.clip(lag, 0, length - 1))
    return jnp.where(lag >= 0, table, jnp.zeros_like(table)) * STEP_MINUTES

def tofts_step(images, aif, ktrans, kep, baseline):
    frames = images.shape[0]
    times = jnp.arange(frames, dtype=jnp.int32).astype(jnp.float32) * STEP_MINUTES
    toeplitz = aif_matrix(aif)
    decay = jnp.exp(-times[:, None] * kep[None, :])
    conc = jnp.dot(toeplitz, decay, precision=lax.Precision.HIGHEST)
    slope = jnp.dot(toeplitz, -times[:, None] * decay, precision=lax.Precision.HIGHEST)
    real_part = images[:, 0]
    imag_part = images[:, 1]
    base_r = baseline[0][None, :]
    base_i = baseline[1][None, :]
    scale = 1.0 + ktrans[None, :] * conc
    miss_r = real_part - base_r * scale
    miss_i = imag_part - base_i * scale
    power = baseline[0] * baseline[0] + baseline[1] * baseline[1]
    project = base_r * miss_r + base_i * miss_i
    h_aa = power * lax.optimization_barrier(jnp.sum(conc * conc, 0))
    h_ab = power * ktrans * lax.optimization_barrier(jnp.sum(conc * slope, 0))
    h_bb = power * ktrans * ktrans * lax.optimization_barrier(jnp.sum(slope * slope, 0))
    g_a = lax.optimization_barrier(jnp.sum(conc * project, 0))
    g_b = ktrans * lax.optimization_barrier(jnp.sum(slope * project, 0))
    d_aa = (1.0 + DAMPING) * h_aa + 1.0
    d_bb = (1.0 + DAMPING) * h_bb + 1.0
    determinant = d_aa * d_bb - h_ab * h_ab
    kt_next = ktrans + (d_bb * g_a - h_ab * g_b) / determinant
    kp_next = kep + (d_aa * g_b - h_ab * g_a) / determinant
    conc_next = jnp.dot(toeplitz, jnp.exp(-times[:, None] * kp_next[None, :]), precision=lax.Precision.HIGHEST)
    scale_next = 1.0 + kt_next[None, :] * conc_next
    residual = jnp.stack([real_part - base_r * scale_next, imag_part - base_i * scale_next], 1)
    return (kt_next, kp_next, residual)

def reference(kspace, sensitivity, spoke_count, spoke_index, band_offset, owner_map, aif, ktrans, kep, baseline):
    column_table, row_table = dft_tables(NX)
    sens = sensitivity.astype(jnp.float32)

    def one_frame(pieces):
        frame_data, count, offset, spoke_number = pieces
        weights = spoke_weights(count, offset, spoke_number, NX)
        grid = jnp.einsum('qxps,cpsy->cqxy', weights, frame_data, preferred_element_type=jnp.float32).astype(jnp.bfloat16)
        half = jnp.einsum('cprk,pkqx->cqrx', grid, column_table, preferred_element_type=jnp.float32).astype(jnp.bfloat16)
        coil_image = jnp.einsum('qypr,cprx->cqyx', row_table, half, preferred_element_type=jnp.float32)
        image_r = lax.optimization_barrier(jnp.sum(sens[:, 0] * coil_image[:, 0] + sens[:, 1] * coil_image[:, 1], 0))
        image_i = lax.optimization_barrier(jnp.sum(sens[:, 0] * coil_image[:, 1] - sens[:, 1] * coil_image[:, 0], 0))
        return jnp.stack([image_r, image_i], 0).astype(jnp.bfloat16)
    images = lax.map(one_frame, (kspace, spoke_count, band_offset, spoke_index))
    flat = images.reshape(FRAMES, 2, N_COILS, SLAB_VOX)
    owned = jnp.take_along_axis(flat, owner_map[None, None], axis=3)
    owned = owned.reshape(FRAMES, 2, N_COILS * SLAB_VOX).astype(jnp.float32)
    kt_next, kp_next, residual = tofts_step(owned, aif, ktrans.reshape(-1), kep.reshape(-1), baseline.reshape(2, -1))
    residual = residual.astype(jnp.bfloat16).reshape(FRAMES, 2, N_COILS, SLAB_VOX)
    slab_rows = jnp.arange(N_COILS, dtype=jnp.int32)[:, None]
    placed = jnp.zeros_like(residual).at[:, :, slab_rows, owner_map].set(residual)
    return (kt_next.reshape(N_COILS, SLAB_VOX), kp_next.reshape(N_COILS, SLAB_VOX), placed.reshape(FRAMES, 2, NX, NX))
```

```python
import functools
import math

import jax
import jax.numpy as jnp
import numpy as np
from jax import lax
from jax.experimental import pallas as pl
from jax.experimental.pallas import tpu as pltpu
from jax.sharding import Mesh
from jax.sharding import PartitionSpec as P

FRAMES = ("frames_0", "frames_1", "frames_2")
STEP_MINUTES = 0.05
DAMPING = 0.1
BF16 = jnp.bfloat16
F32 = jnp.float32
MIB = 1 << 20


def dft_tables(length):
    index = np.arange(length)
    phase = (index[:, None] * index[None, :] % length) * (2.0 * math.pi / length)
    norm = 1.0 / math.sqrt(length)
    return np.stack([np.cos(phase) * norm, np.sin(phase) * norm]).astype(np.float32)


def iota(shape, dim, dtype=jnp.int32):
    return lax.broadcasted_iota(dtype, shape, dim)


def dot(a, b, contract=(1, 0), precision=None):
    return lax.dot_general(
        a,
        b,
        (((contract[0],), (contract[1],)), ((), ())),
        preferred_element_type=F32,
        precision=precision,
    )


def recon_kernel(
    count_ref,
    index_ref,
    offset_ref,
    kspace_hbm,
    sens_hbm,
    table_hbm,
    out_ref,
    kspace,
    sens,
    table,
    columns,
    rows,
    total,
    sems,
):
    coils, _, width = kspace.shape
    spokes = index_ref.shape[1]
    copy_k = pltpu.make_async_copy(kspace_hbm, kspace, sems.at[0])
    copy_t = pltpu.make_async_copy(table_hbm, table, sems.at[1])
    copy_s = [
        pltpu.make_async_copy(sens_hbm.at[c], sens.at[c], sems.at[2 + c]) for c in range(coils)
    ]
    copy_k.start()
    copy_t.start()
    for c in range(coils):
        copy_s[c].start()

    turn = (index_ref[...] * 40503 & 65535).astype(F32) * (2.0 * math.pi / 65536.0)
    live = (iota((1, spokes), 1) < count_ref[0]).astype(F32)
    cosine = live * jnp.cos(turn)
    sine = live * jnp.sin(turn)
    offset = offset_ref[...]
    top = jnp.concatenate([cosine, -sine], 1)
    low = jnp.concatenate([sine, cosine], 1)
    away = iota((width, 2 * spokes), 0) - jnp.concatenate([offset, offset], 1)
    band = jnp.where(
        (away == 0) | (away == 3), 0.25, jnp.where((away == 1) | (away == 2), 0.75, 0.0)
    )
    weights = jnp.concatenate([(band * top).astype(BF16), (band * low).astype(BF16)], 0)

    copy_t.wait()
    tc = table[0]
    ts = table[1]
    columns[:width, :width] = tc
    columns[:width, width:] = ts
    columns[width:, :width] = -ts
    columns[width:, width:] = tc
    rows[:width, :width] = tc
    rows[:width, width:] = -ts
    rows[width:, :width] = ts
    rows[width:, width:] = tc
    copy_k.wait()
    for c in range(coils):
        grid = dot(weights, kspace[c]).astype(BF16)
        half = dot(jnp.concatenate([grid[:width], grid[width:]], 1), columns[...]).astype(BF16)
        image = dot(rows[...], jnp.concatenate([half[:, :width], half[:, width:]], 0))
        copy_s[c].wait()
        sr = sens[c, 0].astype(F32)
        si = sens[c, 1].astype(F32)
        real = sr * image[:width] + si * image[width:]
        imag = sr * image[width:] - si * image[:width]
        if c > 0:
            real = real + total[0]
            imag = imag + total[1]
        if c < coils - 1:
            total[0] = real
            total[1] = imag
        else:
            slabs = out_ref.shape[0]
            deep = width // slabs
            for j in range(slabs):
                out_ref[j, :deep, :] = real[j * deep : (j + 1) * deep].astype(BF16)
                out_ref[j, deep:, :] = imag[j * deep : (j + 1) * deep].astype(BF16)


def recon(count, index, offset, kspace, sens, table, slabs):
    coils, pairs, width = kspace.shape
    vmem = pl.BlockSpec(memory_space=pltpu.VMEM)
    hbm = pl.BlockSpec(memory_space=pl.ANY)
    return pl.pallas_call(
        recon_kernel,
        out_shape=jax.ShapeDtypeStruct((slabs, 2 * width // slabs, width), BF16),
        in_specs=[pl.BlockSpec(memory_space=pltpu.SMEM), vmem, vmem, hbm, hbm, hbm],
        out_specs=vmem,
        scratch_shapes=[
            pltpu.VMEM((coils, pairs, width), BF16),
            pltpu.VMEM((coils, 2, width, width), BF16),
            pltpu.VMEM((2, width, width), BF16),
            pltpu.VMEM((2 * width, 2 * width), BF16),
            pltpu.VMEM((2 * width, 2 * width), BF16),
            pltpu.VMEM((2, width, width), F32),
            pltpu.SemaphoreType.DMA((2 + coils,)),
        ],
        compiler_params=pltpu.CompilerParams(vmem_limit_bytes=24 * MIB),
        name="recon",
    )(count, index, offset, kspace, sens, table)


def prepare_kernel(
    map_ref, aif_ref, ktrans_ref, kep_ref, base_ref, pick_ref, place_ref, slot_row_ref, lag_ref,
    conc_ref, slope_ref, solve_ref,
):
    width, slots = pick_ref.shape
    deep = slots // width
    frames = lag_ref.shape[0]
    row = map_ref[pl.ds(lax.axis_index("coils"), 1), :]
    block = 1024
    inverse = jnp.zeros((2 * deep, width), F32)
    for b in range(0, slots, block):
        part = row[:, b : b + block]
        pick = (iota((width, block), 0) == (part & (width - 1))).astype(F32).astype(BF16)
        pick_ref[:, b : b + block] = pick
        slot = iota((1, block), 1) + b
        here = iota((deep, block), 0) == (part // width)
        high = jnp.where(here, (slot // width).astype(F32), 0.0)
        low = jnp.where(here, (slot & (width - 1)).astype(F32), 0.0)
        digits = jnp.concatenate([high, low], 0).astype(BF16)
        inverse = inverse + dot(digits, pick, (1, 1))
    slot_row_ref[...] = inverse[:deep]
    low = inverse[deep:].astype(jnp.int32)
    for y in range(deep):
        place = (iota((width, width), 0) == low[y : y + 1]).astype(F32).astype(BF16)
        place_ref[:, y * width : (y + 1) * width] = place

    spread = jnp.broadcast_to(aif_ref[...], (frames, aif_ref.shape[1]))
    shifted = pltpu.roll(spread, 0, 1, stride=1, stride_axis=0)[:, :frames]
    early = iota((frames, frames), 1) >= iota((frames, frames), 0)
    lag = jnp.where(early, shifted, 0.0).T * STEP_MINUTES
    lag_ref[...] = lag
    times = iota((frames, 1), 0).astype(F32) * STEP_MINUTES
    ktrans = ktrans_ref[...]
    kep = kep_ref[...]
    decay = jnp.exp(-times * kep)
    conc = dot(lag, decay, precision=lax.Precision.HIGHEST)
    slope = dot(lag, -times * decay, precision=lax.Precision.HIGHEST)
    conc_ref[...] = conc
    slope_ref[...] = slope
    base_r = base_ref[0]
    base_i = base_ref[1]
    power = base_r * base_r + base_i * base_i
    h_aa = power * jnp.sum(conc * conc, 0, keepdims=True)
    h_ab = power * ktrans * jnp.sum(conc * slope, 0, keepdims=True)
    h_bb = power * ktrans * ktrans * jnp.sum(slope * slope, 0, keepdims=True)
    d_aa = (1.0 + DAMPING) * h_aa + 1.0
    d_bb = (1.0 + DAMPING) * h_bb + 1.0
    solve_ref[0:1, :] = d_aa
    solve_ref[1:2, :] = d_bb
    solve_ref[2:3, :] = h_ab
    solve_ref[3:4, :] = d_aa * d_bb - h_ab * h_ab


def prepare(owner_map, aif, ktrans, kep, baseline, width):
    slots = owner_map.shape[1]
    frames = aif.shape[0]
    own = ktrans.shape[1]
    lanes = -(-frames // 128) * 128
    aif_row = jnp.pad(aif, (0, lanes - frames)).reshape(1, lanes)
    vmem = pl.BlockSpec(memory_space=pltpu.VMEM)
    return pl.pallas_call(
        prepare_kernel,
        out_shape=(
            jax.ShapeDtypeStruct((width, slots), BF16),
            jax.ShapeDtypeStruct((width, slots), BF16),
            jax.ShapeDtypeStruct((slots // width, width), F32),
            jax.ShapeDtypeStruct((frames, frames), F32),
            jax.ShapeDtypeStruct((frames, own), F32),
            jax.ShapeDtypeStruct((frames, own), F32),
            jax.ShapeDtypeStruct((8, own), F32),
        ),
        in_specs=[vmem] * 5,
        out_specs=(vmem,) * 7,
        compiler_params=pltpu.CompilerParams(vmem_limit_bytes=24 * MIB),
        cost_estimate=pl.CostEstimate(flops=10**9, bytes_accessed=9 * MIB, transcendentals=10**4),
        name="prepare",
    )(owner_map, aif_row, ktrans, kep, baseline)


def pick_kernel(parts_ref, map_ref, pick_ref, out_ref, lines):
    width, slots = pick_ref.shape
    deep = slots // width
    lanes = out_ref.shape[1]
    total = parts_ref[0].astype(F32)
    for c in range(1, parts_ref.shape[0]):
        total = total + parts_ref[c].astype(F32)
    image = total.astype(BF16)
    row = map_ref[pl.ds(lax.axis_index("coils"), 1), :] // width
    block = 1024
    for b in range(0, slots, block):
        table = dot(image, pick_ref[:, b : b + block])
        here = iota((deep, block), 0) == row[:, b : b + block]
        for part in range(2):
            value = jnp.where(here, table[part * deep : (part + 1) * deep], 0.0)
            line = jnp.sum(value, 0, keepdims=True)
            for n in range(block // lanes):
                at = 2 * (b // lanes + n) + part
                lines[at : at + 1, :] = line[:, n * lanes : (n + 1) * lanes]
    out_ref[...] = lines[...].astype(BF16)


def pick_slots(parts, owner_map, pick, lanes):
    slots = owner_map.shape[1]
    vmem = pl.BlockSpec(memory_space=pltpu.VMEM)
    return pl.pallas_call(
        pick_kernel,
        out_shape=jax.ShapeDtypeStruct((2 * slots // lanes, lanes), BF16),
        in_specs=[vmem] * 3,
        out_specs=vmem,
        scratch_shapes=[pltpu.VMEM((2 * slots // lanes, lanes), F32)],
        compiler_params=pltpu.CompilerParams(vmem_limit_bytes=24 * MIB),
        name="pick",
    )(parts, owner_map, pick)


def step_kernel(
    owned_ref, lag_ref, conc_ref, slope_ref, solve_ref, ktrans_ref, kep_ref, base_ref,
    ktrans_out, kep_out, out_ref, lines,
):
    frames = lag_ref.shape[0]
    lines[...] = owned_ref[...].astype(F32)
    real = lines[pl.ds(0, frames, stride=2), :]
    imag = lines[pl.ds(1, frames, stride=2), :]
    ktrans = ktrans_ref[...]
    kep = kep_ref[...]
    base_r = base_ref[0]
    base_i = base_ref[1]
    conc = conc_ref[...]
    slope = slope_ref[...]
    scale = 1.0 + ktrans * conc
    project = base_r * (real - base_r * scale) + base_i * (imag - base_i * scale)
    g_a = jnp.sum(conc * project, 0, keepdims=True)
    g_b = ktrans * jnp.sum(slope * project, 0, keepdims=True)
    d_aa = solve_ref[0:1, :]
    d_bb = solve_ref[1:2, :]
    h_ab = solve_ref[2:3, :]
    determinant = solve_ref[3:4, :]
    kt_next = ktrans + (d_bb * g_a - h_ab * g_b) / determinant
    kp_next = kep + (d_aa * g_b - h_ab * g_a) / determinant
    ktrans_out[...] = kt_next
    kep_out[...] = kp_next
    times = iota((frames, 1), 0).astype(F32) * STEP_MINUTES
    decay = jnp.exp(-times * kp_next)
    scale = 1.0 + kt_next * dot(lag_ref[...], decay, precision=lax.Precision.HIGHEST)
    lines[pl.ds(0, frames, stride=2), :] = real - base_r * scale
    lines[pl.ds(1, frames, stride=2), :] = imag - base_i * scale
    out_ref[...] = lines[...].astype(BF16)


def tofts_step(owned, model, ktrans, kep, baseline):
    own = ktrans.shape[1]
    vmem = pl.BlockSpec(memory_space=pltpu.VMEM)
    return pl.pallas_call(
        step_kernel,
        out_shape=(
            jax.ShapeDtypeStruct((1, own), F32),
            jax.ShapeDtypeStruct((1, own), F32),
            jax.ShapeDtypeStruct(owned.shape, BF16),
        ),
        in_specs=[vmem] * 8,
        out_specs=(vmem,) * 3,
        scratch_shapes=[pltpu.VMEM(owned.shape, F32)],
        compiler_params=pltpu.CompilerParams(vmem_limit_bytes=8 * MIB),
        name="step",
    )(owned, *model, ktrans, kep, baseline)


def place_kernel(returned_ref, place_ref, slot_row_ref, out_ref, lines, image):
    width, slots = place_ref.shape
    deep = slots // width
    lines[...] = returned_ref[...].astype(F32)
    halves = [
        [lines[pl.ds(part + 2 * side, deep, stride=4), :] for side in range(2)] for part in range(2)
    ]
    source = jnp.concatenate([jnp.concatenate(h, 1) for h in halves], 0).astype(BF16)
    across = 4
    for y in range(0, deep, across):
        table = dot(source, place_ref[:, y * width : (y + across) * width])
        for n in range(across):
            which = slot_row_ref[y + n : y + n + 1, :]
            here = iota((deep, width), 0).astype(F32) == which
            for part in range(2):
                values = table[part * deep : (part + 1) * deep, n * width : (n + 1) * width]
                line = jnp.sum(jnp.where(here, values, 0.0), 0, keepdims=True)
                image[part * deep + y + n : part * deep + y + n + 1, :] = line
    out_ref[...] = image[...].astype(BF16)


def place_voxels(returned, place, slot_row):
    width, slots = place.shape
    deep = slots // width
    vmem = pl.BlockSpec(memory_space=pltpu.VMEM)
    return pl.pallas_call(
        place_kernel,
        out_shape=jax.ShapeDtypeStruct((2 * deep, width), BF16),
        in_specs=[vmem] * 3,
        out_specs=vmem,
        scratch_shapes=[pltpu.VMEM(returned.shape, F32), pltpu.VMEM((2 * deep, width), F32)],
        compiler_params=pltpu.CompilerParams(vmem_limit_bytes=24 * MIB),
        name="place",
    )(returned, place, slot_row)


def shards(
    kspace,
    sensitivity,
    spoke_count,
    spoke_index,
    band_offset,
    owner_map,
    aif,
    ktrans,
    kep,
    baseline,
    table,
):
    _, coils, _, spokes, width = kspace.shape
    slabs = lax.axis_size("coils")
    own = ktrans.shape[1]
    parts = recon(
        spoke_count,
        spoke_index,
        band_offset,
        kspace.reshape(coils, 2 * spokes, width),
        sensitivity,
        table,
        slabs,
    )
    parts = lax.all_to_all(parts, "coils", 0, 0, tiled=True)
    pick, place, slot_row, *model = prepare(owner_map, aif, ktrans, kep, baseline, width)
    picked = pick_slots(parts, owner_map, pick, own)
    owned = lax.all_to_all(picked.reshape(-1, 2, own), FRAMES, 0, 0, tiled=True)
    kt_next, kp_next, residual = tofts_step(owned.reshape(-1, own), model, ktrans, kep, baseline)
    returned = lax.all_to_all(residual.reshape(-1, 2, own), FRAMES, 0, 0, tiled=True)
    placed = place_voxels(returned.reshape(-1, own), place, slot_row)
    return kt_next, kp_next, placed.reshape(1, 2, width // slabs, width)


def solution(mesh):
    split = Mesh(
        mesh.devices.reshape(8, 4, 2, mesh.shape["coils"]),
        ("frames_0", "frames_1", "frames_2", "coils"),
    )
    placed = (
        P(FRAMES, "coils", None, None, None),
        P("coils", None, None, None),
        P(FRAMES),
        P(FRAMES, None),
        P(FRAMES, None),
        P(),
        P(),
        P("coils", FRAMES),
        P("coils", FRAMES),
        P(None, "coils", FRAMES),
    )
    mapped = jax.shard_map(
        shards,
        mesh=split,
        in_specs=(*placed, P()),
        out_specs=(P("coils", FRAMES), P("coils", FRAMES), P(FRAMES, None, "coils", None)),
        check_vma=False,
    )

    def step(kspace, *rest):
        table = jnp.asarray(dft_tables(kspace.shape[-1])).astype(BF16)
        return mapped(kspace, *rest, table)

    return step
```
